256 devices in a mesh: row: 8 (over z_hi, core), col: 32 (over x, z_lo, y).
Axes of the slice: x: 4, y: 4, z: 8 (z_hi: 4, z_lo: 2; z = z_hi * 2 + z_lo), core: 2. Of those that a mesh axis runs over, the one named last changes fastest.
Arguments:
- basis_out: float32 [16384, 16384], P('row', 'col'), may hold values from -0.046875 to 0.046875
- basis_in: float32 [16384, 16384], P('col', 'row'), may hold values from -0.046875 to 0.046875
- eig_damped: float32 [16384, 16384], P('col', 'row'), may hold values from 0.5 to 8
- query_left: bfloat16 [16384, 256], P(('row', 'col')), may hold values from -0.375 to 0.375
- query_right: bfloat16 [16384, 256], P('col'), may hold values from -6 to 6
- train_left: bfloat16 [16384, 512], P(('row', 'col')), may hold values from -0.046875 to 0.046875
- train_right: bfloat16 [16384, 512], P('col'), may hold values from -0.046875 to 0.046875
Outputs:
- response: float32 [16384, 512], P(('row', 'col'))
- scores: float32 [512], replicated
The draws below stay inside these ranges and needn't reach their ends.
All inputs are finite; a program needn't handle non-finite values.
Results may differ from the reference program's by a relative error of at most 0.0003.
Values may be sent and summed in bfloat16 or wider, within the bound.
No kernel may reach another device: no remote copies, remote signals or barrier semaphores. Data moves between devices by JAX's collectives and lax.ppermute only.
A program may use at most 128 MiB of HBM per device.

```python
import math
import jax
import jax.numpy as jnp
from jax import lax

D_OUT = 16384
D_IN = 16384
RANK = 256
TRAIN = 512


def block_levels(key, dims, shards, least, largest):
    def one(position, shards_of):
        heights = jax.random.uniform(jax.random.fold_in(jax.random.fold_in(key, 6), position), (shards_of,), jnp.float32, least / len(shards), largest / len(shards))
        return jnp.repeat(jnp.exp(heights), dims[position] // shards_of).reshape((-1,) + (1,) * (len(dims) - position - 1))

    loudness = one(*shards[0])
    for cut in shards[1:]:
        loudness = loudness * one(*cut)
    return loudness


def bell_draw(stream_key, shape, deviation, bound, pieces=(), held_as=jnp.bfloat16):
    values = jax.random.normal(stream_key, shape, jnp.float32) * deviation
    if len(pieces) > 0:
        values = block_levels(stream_key, shape, pieces, -0.22, 0.18) * values
    return jnp.clip(values, min=-bound, max=bound).astype(held_as)


def setup_inputs(seed: int = 0) -> dict:
    arg_keys = jax.random.split(jax.random.key(seed), 8)
    return {
        "basis_out": bell_draw(arg_keys[0], (D_OUT, D_OUT), D_OUT ** -0.5, 0.046875, ((0, 8), (1, 32)), jnp.float32),
        "basis_in": bell_draw(arg_keys[1], (D_IN, D_IN), D_IN ** -0.5, 0.046875, ((0, 32), (1, 8)), jnp.float32),
        "eig_damped": jnp.clip(jnp.exp(math.log(8.0) - 2.7725887 * jax.random.uniform(arg_keys[2], (D_OUT, D_IN), jnp.float32) ** block_levels(arg_keys[2], (D_OUT, D_IN), ((0, 32), (1, 8)), -0.2, 0.2)), 0.5, 8.0),
        "query_left": bell_draw(arg_keys[3], (D_OUT, RANK), RANK ** -0.5, 0.375, ((0, 256),)),
        "query_right": bell_draw(arg_keys[4], (D_IN, RANK), 1.0, 6.0, ((0, 32),)),
        "train_left": bell_draw(arg_keys[5], (D_OUT, TRAIN), D_OUT ** -0.5, 0.046875, ((0, 256),)),
        "train_right": bell_draw(arg_keys[6], (D_IN, TRAIN), D_IN ** -0.5, 0.046875, ((0, 32),)),
    }


def dot_first(left, right):
    return lax.dot_general(left, right, (((0,), (0,)), ((), ())), precision=lax.Precision.HIGHEST, preferred_element_type=jnp.float32)


def dot_last(left, right):
    return lax.dot_general(left, right, (((1,), (1,)), ((), ())), precision=lax.Precision.HIGHEST, preferred_element_type=jnp.float32)


def reference(basis_out, basis_in, eig_damped, query_left, query_right, train_left, train_right):
    rot_left = dot_first(basis_out, query_left.astype(jnp.float32))
    rot_right = dot_first(basis_in, query_right.astype(jnp.float32))
    rot_train = dot_first(basis_in, train_right.astype(jnp.float32))

    def one_block(index):
        first = (index * 256).astype(jnp.int32)
        left_rows = lax.dynamic_slice_in_dim(rot_left, first, 256, 0)
        eigen_rows = lax.dynamic_slice_in_dim(eig_damped, first, 256, 0)
        precond = dot_last(left_rows, rot_right) / eigen_rows
        return jnp.dot(precond, rot_train, precision=lax.Precision.HIGHEST, preferred_element_type=jnp.float32)

    applied = lax.map(one_block, jnp.arange(D_OUT // 256, dtype=jnp.int32)).reshape(D_OUT, TRAIN)
    response = jnp.dot(basis_out, applied, precision=lax.Precision.HIGHEST, preferred_element_type=jnp.float32)
    scores = jnp.sum(train_left.astype(jnp.float32) * response, axis=0)
    return response, scores
```

```python
import jax
import jax.numpy as jnp
from jax import lax
from jax.experimental import pallas as pl
from jax.experimental.pallas import tpu as pltpu
from jax.sharding import Mesh
from jax.sharding import PartitionSpec as P

COL = ("col_0", "col_1", "col_2")
ROW = ("row_0", "row_1")
ROW_COL = ROW + COL

SPAN = 250.0
HALF = 125.0
SHARE = 64
f32, bf16 = jnp.float32, jnp.bfloat16


def exchange(pieces, axis):
    return lax.all_to_all(pieces, axis, split_axis=0, concat_axis=0, tiled=True)


def to_everyone(array, axis):
    return exchange(jnp.broadcast_to(array, (lax.axis_size(axis), *array.shape)), axis)


def ring(axis, step):
    n = lax.axis_size(axis)
    return [(k, (k + step) % n) for k in range(n)]


def levels_of(block, axis):
    most = jnp.max(jnp.abs(block), axis=axis, keepdims=True)
    level = jnp.ceil(jnp.log2(jnp.maximum(most, 1e-36)) * 8.0) * 0.125
    return level, jnp.floor(level)


def code_of(block, level):
    size = jnp.exp2(jnp.abs(block) * (jnp.exp2(-level) * SPAN) - HALF)
    return jnp.where(block < 0, -size, size).astype(bf16)


def value_of(code, scale):
    code = code.astype(f32)
    size = (jnp.log2(jnp.abs(code)) + HALF) * scale
    return jnp.where(code < 0, -size, size)


def put_blocks(out, lead, parts):
    rows = jnp.zeros((16, 128), f32)
    at = lax.broadcasted_iota(jnp.int32, (16, 128), 0)
    for k, part in enumerate(parts):
        level, first = levels_of(part, 0)
        out[lead, pl.ds(k * SHARE, SHARE), :] = code_of(part, level)
        rows = jnp.where(at == k, first, rows)
        rows = jnp.where(at == k + 8, level - first, rows)
    out[lead, pl.ds(len(parts) * SHARE, 16), :] = rows.astype(bf16)


def message_of(blocks):
    level, first = levels_of(blocks, 1)
    code = code_of(blocks, level).reshape(-1, 128)
    pad = ((0, 8 - blocks.shape[0]), (0, 0))
    rows = [jnp.pad(a[:, 0], pad).astype(bf16) for a in (first, level - first)]
    return jnp.concatenate([code, *rows], axis=0)


def sum_of(got):
    n = got.shape[1] // SHARE
    level = got[:, n * SHARE : n * SHARE + n].astype(f32) + got[:, -8 : n - 8].astype(f32)
    scale = jnp.exp2(level)[:, :, None] * (1.0 / SPAN)
    return jnp.sum(value_of(got[:, : n * SHARE].reshape(-1, n, SHARE, 128), scale), axis=0)


def halves(array):
    high = array.astype(bf16)
    return high, (array - high.astype(f32)).astype(bf16)


def split(array):
    high = lax.reduce_precision(array, 8, 7)
    return high.astype(bf16), (array - high).astype(bf16)


def multiply(left, right, dims):
    return lax.dot_general(left, right, (dims, ((), ())), preferred_element_type=f32)


FIRST, PLAIN, LAST = ((0,), (0,)), ((1,), (0,)), ((1,), (1,))


def call(kernel, out, grid, ins, outs, args, flops, vmem, scratch=()):
    size = sum(a.size * a.dtype.itemsize for a in args)
    return pl.pallas_call(
        kernel,
        out_shape=out,
        grid=(grid,),
        in_specs=ins,
        out_specs=outs,
        scratch_shapes=scratch,
        cost_estimate=pl.CostEstimate(flops=flops, transcendentals=0, bytes_accessed=size),
        compiler_params=pltpu.CompilerParams(vmem_limit_bytes=vmem * 2**20),
        name=kernel.__name__,
    )(*args)


def whole(shape):
    return pl.BlockSpec(shape, lambda i: (0,) * len(shape))


def blocks(shape, dim):
    return pl.BlockSpec(shape, lambda i: tuple(i if k == dim else 0 for k in range(len(shape))))


def rotate_in(basis, given, out):
    right = jnp.concatenate(halves(basis[...]), axis=0)
    n = out.shape[1] // SHARE
    for h in range(2):
        rows = slice(h * n * SHARE, (h + 1) * n * SHARE)
        turned = multiply(given[rows, :], right, PLAIN)
        for d in range(out.shape[0] // 2):
            cut = slice(d * 128, (d + 1) * 128)
            put_blocks(
                out, 2 * d + h, [turned[k * SHARE : (k + 1) * SHARE, cut] for k in range(n)]
            )


def apply_piece(got, left, eig, out, right, other):
    n = got.shape[1] // SHARE
    tall = right.shape[0] // 3

    @pl.when(pl.program_id(0) == 0)
    def _():
        out[...] = jnp.zeros_like(out)

    for d in range(got.shape[0]):
        rows = got[d, pl.ds(n * SHARE, 16), :].astype(f32)
        lanes = pl.ds((d // 2) * 128, 128)
        for k in range(n):
            scale = jnp.exp2(rows[k : k + 1] + rows[k + 8 : k + 9]) * (1.0 / SPAN)
            high, low = halves(value_of(got[d, pl.ds(k * SHARE, SHARE), :], scale))
            at = ((d % 2) * n + k) * SHARE
            if at < tall:
                right[pl.ds(at, SHARE), lanes] = high
                right[pl.ds(tall + at, SHARE), lanes] = high
                right[pl.ds(2 * tall + at, SHARE), lanes] = low
            else:
                at = pl.ds(at - tall, SHARE)
                wide = eig.shape[1]
                other[at, lanes] = high
                other[at, pl.ds(wide + (d // 2) * 128, 128)] = high
                other[at, pl.ds(2 * wide + (d // 2) * 128, 128)] = low
    high, low = halves(multiply(left[...], right[...], PLAIN) / eig[...])
    out[...] += multiply(jnp.concatenate([high, low, high], axis=1), other[...], LAST)


def respond(basis, given, out):
    high, low = halves(basis[...])
    partial = multiply(jnp.concatenate([high, low, high], axis=1), given[...], PLAIN)
    n = partial.shape[1] // 128
    for d in range(out.shape[0]):
        rows = slice(d * SHARE, (d + 1) * SHARE)
        put_blocks(out, d, [partial[rows, k * 128 : (k + 1) * 128] for k in range(n)])


def my_half_summed(array):
    core = lax.axis_index("row_1")
    rows = array.shape[0] // 2
    mine = lax.dynamic_slice_in_dim(array, core * rows, rows, 0)
    other = lax.dynamic_slice_in_dim(array, (1 - core) * rows, rows, 0)
    return mine + lax.ppermute(other, "row_1", ring("row_1", 1))


def both_halves(half):
    core = lax.axis_index("row_1")
    other = lax.ppermute(half, "row_1", ring("row_1", 1))
    return jnp.where(
        core == 0, jnp.concatenate([half, other], 0), jnp.concatenate([other, half], 0)
    )


def summed_over_chips(array):
    rows, cols = array.shape
    blocks_ = array.reshape(rows // SHARE, SHARE, cols)
    most = jnp.max(jnp.abs(blocks_), axis=1, keepdims=True)
    level = jnp.ceil(jnp.log2(jnp.maximum(most, 1e-36)) * 8.0) * 0.125
    code = code_of(blocks_, level).reshape(rows, cols)
    first = jnp.floor(level)
    levels = jnp.concatenate([first, level - first], axis=1)
    levels = jnp.concatenate([levels, jnp.zeros((rows // SHARE, 14, cols), f32)], axis=1)
    message = jnp.concatenate([code, levels.reshape(-1, cols).astype(bf16)], axis=0)
    total = array
    for step in (2, 1, 3):
        got = lax.ppermute(message, "row_0", ring("row_0", step))
        level = got[rows:].reshape(rows // SHARE, 16, cols)[:, :2].astype(f32)
        scale = jnp.exp2(jnp.sum(level, axis=1, keepdims=True)) * (1.0 / SPAN)
        total += value_of(got[:rows].reshape(blocks_.shape), scale).reshape(rows, cols)
    return total


def body(basis_out, basis_in, eig_damped, query_left, query_right, train_left, train_right):
    cols = lax.axis_size(COL)
    rank, train = query_right.shape[1], train_right.shape[1]
    n_out, n_in = eig_damped.shape
    struct = jax.ShapeDtypeStruct

    query = to_everyone(query_left, COL)
    step = 4
    n = (rank + train) // 128
    height = n * SHARE + 16
    wide = step // 2 * 128
    given = jnp.concatenate([query_right, train_right], axis=1).T
    given = jnp.concatenate([given, given], axis=1)
    message = call(
        rotate_in,
        pltpu.VMEM((cols, height, 128), bf16),
        cols // step,
        [blocks((basis_in.shape[0], wide), 1), whole(given.shape)],
        blocks((step, height, 128), 0),
        (basis_in, given),
        4 * basis_in.size * (rank + train),
        16,
    )
    message, query = lax.optimization_barrier((message, query))
    got = exchange(message, COL)

    high, low = split(basis_out)
    query = query.reshape(-1, rank)
    rot_left = multiply(high, query, FIRST) + multiply(low, query, FIRST)
    rot_left = both_halves(summed_over_chips(my_half_summed(rot_left)))
    high, low = split(rot_left)
    left = jnp.concatenate([high, low, high], axis=1)

    got = to_everyone(message_of(sum_of(got)), COL)
    contrib = call(
        apply_piece,
        struct((n_out, train), f32),
        cols // step,
        [
            blocks((step, height, 128), 0),
            whole(left.shape),
            blocks((n_out, wide), 1),
        ],
        whole((n_out, train)),
        (got, left, eig_damped),
        6 * eig_damped.size * (rank + train),
        24,
        [pltpu.VMEM((3 * rank, wide), bf16), pltpu.VMEM((train, 3 * wide), bf16)],
    )
    applied = both_halves(summed_over_chips(my_half_summed(contrib)))
    high, low = split(applied)
    given = jnp.concatenate([high, high, low], axis=0)

    n = train // 128
    height = n * SHARE + 16
    message = call(
        respond,
        pltpu.VMEM((cols, height, 128), bf16),
        cols // step,
        [blocks((step * SHARE, n_out), 0), whole(given.shape)],
        blocks((step, height, 128), 0),
        (basis_out, given),
        6 * basis_out.size * train,
        16,
    )
    response = sum_of(exchange(message, COL))
    response = jnp.concatenate([response[k] for k in range(n)], axis=1)
    scores = jnp.sum(train_left.astype(f32) * response, axis=0).reshape(-1, 128)
    scores = jnp.sum(to_everyone(scores, COL), axis=0)
    scores = jnp.sum(to_everyone(scores, ROW), axis=0)
    return response, scores.reshape(-1)


def solution(mesh):
    finer = Mesh(mesh.devices.reshape(4, 2, 4, 2, 4), ROW_COL)
    placed = (
        P(ROW, COL),
        P(COL, ROW),
        P(COL, ROW),
        P(ROW_COL, None),
        P(COL, None),
        P(ROW_COL, None),
        P(COL, None),
    )
    return jax.shard_map(
        body, mesh=finer, in_specs=placed, out_specs=(P(ROW_COL, None), P()), check_vma=False
    )
```

```python
import jax
import jax.numpy as jnp
from jax import lax
from jax.experimental import pallas as pl
from jax.experimental.pallas import tpu as pltpu
from jax.sharding import Mesh
from jax.sharding import PartitionSpec as P

COL = ("col_0", "col_1", "col_2")
ROW = ("row_0", "row_1")
ROW_COL = ROW + COL


SPAN = 250.0
HALF = 125.0
SHARE = 64
f32, bf16 = jnp.float32, jnp.bfloat16


def exchange(pieces, axis):
    return lax.all_to_all(pieces, axis, split_axis=0, concat_axis=0, tiled=True)


def to_everyone(array, axis):
    return exchange(jnp.broadcast_to(array, (lax.axis_size(axis), *array.shape)), axis)


def ring(axis, step):
    n = lax.axis_size(axis)
    return [(k, (k + step) % n) for k in range(n)]


def tail_of(n):
    return 8 if n <= 4 else 16


def levels_of(block, axis):
    most = jnp.max(jnp.abs(block), axis=axis, keepdims=True)
    level = jnp.ceil(jnp.log2(jnp.maximum(most, 1e-36)) * 8.0) * 0.125
    return level, jnp.floor(level)


def code_of(block, level):
    size = jnp.exp2(jnp.abs(block) * (jnp.exp2(-level) * SPAN) - HALF)
    return jnp.where(block < 0, -size, size).astype(bf16)


def value_of(code, scale):
    code = code.astype(f32)
    size = (jnp.log2(jnp.abs(code)) + HALF) * scale
    return jnp.where(code < 0, -size, size)


def put_blocks(out, lead, parts, plain=()):
    tail = tail_of(len(parts))
    out = out.at[lead]
    rows = jnp.zeros((tail, 128), f32)
    at = lax.broadcasted_iota(jnp.int32, (tail, 128), 0)
    for k, part in enumerate(parts):
        level, first = levels_of(part, 0)
        out[pl.ds(k * SHARE, SHARE), :] = code_of(part, level)
        rows = jnp.where(at == k, first, rows)
        rows = jnp.where(at == k + tail // 2, level - first, rows)
    for k, part in enumerate(plain):
        out[pl.ds((len(parts) + k) * SHARE, SHARE), :] = part
    out[pl.ds(out.shape[0] - tail, tail), :] = rows.astype(bf16)


def message_of(blocks):
    level, first = levels_of(blocks, 1)
    code = code_of(blocks, level).reshape(-1, 128)
    pad = ((0, tail_of(blocks.shape[0]) // 2 - blocks.shape[0]), (0, 0))
    rows = [jnp.pad(a[:, 0], pad).astype(bf16) for a in (first, level - first)]
    return jnp.concatenate([code, *rows], axis=0)


def sum_of(got, n):
    at = got.shape[1] - tail_of(n)
    half = at + tail_of(n) // 2
    level = got[:, at : at + n].astype(f32) + got[:, half : half + n].astype(f32)
    scale = jnp.exp2(level)[:, :, None] * (1.0 / SPAN)
    return jnp.sum(value_of(got[:, : n * SHARE].reshape(-1, n, SHARE, 128), scale), axis=0)


def halves(array):
    high = array.astype(bf16)
    return high, (array - high.astype(f32)).astype(bf16)


def split(array):
    high = lax.reduce_precision(array, 8, 7)
    return high.astype(bf16), (array - high).astype(bf16)


def multiply(left, right, dims):
    return lax.dot_general(left, right, (dims, ((), ())), preferred_element_type=f32)


FIRST, PLAIN, LAST = ((0,), (0,)), ((1,), (0,)), ((1,), (1,))


def call(kernel, out, grid, ins, outs, args, flops, vmem, scratch=()):
    size = sum(a.size * a.dtype.itemsize for a in args)
    return pl.pallas_call(
        kernel,
        out_shape=out,
        grid=(grid,),
        in_specs=ins,
        out_specs=outs,
        scratch_shapes=scratch,
        cost_estimate=pl.CostEstimate(flops=flops, transcendentals=0, bytes_accessed=size),
        compiler_params=pltpu.CompilerParams(vmem_limit_bytes=vmem * 2**20),
    )(*args)


def whole(shape):
    return pl.BlockSpec(shape, lambda i: (0,) * len(shape))


def blocks(shape, dim):
    return pl.BlockSpec(shape, lambda i: tuple(i if k == dim else 0 for k in range(len(shape))))


OFFSETS = (0, 3, 1, 2)


def around(array, axis):
    return [array] + [lax.ppermute(array, axis, ring(axis, 4 - k)) for k in OFFSETS[1:]]


def rotate_in(basis, given, query, out):
    right = jnp.concatenate(halves(basis[...]), axis=0)
    n = given.shape[0] // (2 * SHARE)
    plain = [query[:, k * 128 : (k + 1) * 128] for k in range(query.shape[1] // 128)]
    for h in range(2):
        rows = slice(h * n * SHARE, (h + 1) * n * SHARE)
        turned = multiply(given[rows, :], right, PLAIN)
        for d in range(out.shape[2]):
            cut = slice(d * 128, (d + 1) * 128)
            parts = [turned[k * SHARE : (k + 1) * SHARE, cut] for k in range(n)]
            put_blocks(out, (0, h, d), parts, plain)


def apply_piece(place, left, eig, *refs):
    firsts, seconds, (out, right, other, shares, done) = refs[:4], refs[4:8], refs[8:]
    n = (firsts[0].shape[1] - 16) // SHARE
    tall = right.shape[1] // 3
    copies = []
    for s in range(8):
        for t in range(2):
            group = lax.rem(place[0] + OFFSETS[s // 2], 4) * 4
            group += lax.rem(place[1] + OFFSETS[s % 2 * 2 + t], 4)
            lanes = pl.ds(pl.multiple_of(group * 128, 128), 128)
            into = shares.at[s, :, pl.ds(t * 128, 128)]
            copies.append(pltpu.make_async_copy(eig.at[:, lanes], into, done.at[s * 2 + t]))
            copies[-1].start()
    out[...] = jnp.zeros_like(out)
    for s in range(8):
        a, slot = s // 2, s % 2
        for t in range(2):
            b = s % 2 * 2 + t
            lanes = pl.ds(t * 128, 128)
            for h, got in enumerate((firsts[b].at[a], seconds[a].at[b])):
                rows = got[pl.ds(n * SHARE, 16), :].astype(f32)
                for k in range(n):
                    scale = jnp.exp2(rows[k : k + 1] + rows[k + 8 : k + 9]) * (1.0 / SPAN)
                    high, low = halves(value_of(got[pl.ds(k * SHARE, SHARE), :], scale))
                    at = (h * n + k) * SHARE
                    if at < tall:
                        right[slot, pl.ds(at, SHARE), lanes] = high
                        right[slot, pl.ds(tall + at, SHARE), lanes] = high
                        right[slot, pl.ds(2 * tall + at, SHARE), lanes] = low
                    else:
                        at = pl.ds(at - tall, SHARE)
                        other[slot, at, lanes] = high
                        other[slot, at, pl.ds(256 + t * 128, 128)] = high
                        other[slot, at, pl.ds(512 + t * 128, 128)] = low
        copies[2 * s].wait()
        copies[2 * s + 1].wait()
        precond = multiply(left[...], right[slot], PLAIN) / shares[s]
        high, low = halves(precond)
        out[...] += multiply(jnp.concatenate([high, low, high], axis=1), other[slot], LAST)


def respond(basis, given, out):
    high, low = halves(basis[...])
    partial = multiply(jnp.concatenate([high, low, high], axis=1), given[...], PLAIN)
    n = partial.shape[1] // 128
    for d in range(out.shape[0]):
        rows = slice(d * SHARE, (d + 1) * SHARE)
        put_blocks(out, d, [partial[rows, k * 128 : (k + 1) * 128] for k in range(n)])


def my_half_summed(array):
    core = lax.axis_index("row_1")
    rows = array.shape[0] // 2
    mine = lax.dynamic_slice_in_dim(array, core * rows, rows, 0)
    other = lax.dynamic_slice_in_dim(array, (1 - core) * rows, rows, 0)
    return mine + lax.ppermute(other, "row_1", ring("row_1", 1))


def both_halves(half):
    core = lax.axis_index("row_1")
    other = lax.ppermute(half, "row_1", ring("row_1", 1))
    return jnp.where(
        core == 0, jnp.concatenate([half, other], 0), jnp.concatenate([other, half], 0)
    )


def coded_columns(array, tail):
    cols = array.shape[1]
    parts = array.reshape(-1, SHARE, cols)
    level, first = levels_of(parts, 1)
    rows = [code_of(parts, level), first.astype(bf16), (level - first).astype(bf16)]
    rows.append(jnp.zeros((parts.shape[0], tail - 2, cols), bf16))
    return jnp.concatenate(rows, axis=1)


def column_values(message):
    level = message[:, SHARE].astype(f32) + message[:, SHARE + 1].astype(f32)
    return value_of(message[:, :SHARE], jnp.exp2(level)[:, None] * (1.0 / SPAN))


def summed_over_chips(array, after):
    message, _ = lax.optimization_barrier((coded_columns(array, 8), after))
    arrived = [lax.ppermute(message, "row_0", ring("row_0", step)) for step in (1, 3, 2)]
    total = array
    for got in arrived:
        total += column_values(got).reshape(array.shape)
    return total


def summed_in_turn(array):
    me = lax.axis_index("row_0")
    chips = lax.axis_size("row_0")
    message = coded_columns(array, 8)
    total = lax.dynamic_slice_in_dim(array, me * SHARE, SHARE, 0)
    arrived = []
    for step in (1, 3, 2):
        piece = lax.dynamic_index_in_dim(message, lax.rem(me + step, chips), 0)
        arrived.append(lax.ppermute(piece, "row_0", ring("row_0", step)))
    for got in arrived:
        total += column_values(got)[0]
    pieces = lax.all_gather(coded_columns(total, 8), "row_0", axis=0, tiled=True)
    return column_values(pieces).reshape(array.shape)


def respond_to(basis_out, applied):
    cols = lax.axis_size(COL)
    n_out, train = applied.shape
    high, low = split(applied)
    given = jnp.concatenate([high, high, low], axis=0)
    n = train // 128
    height = n * SHARE + tail_of(n)
    step = 4
    message = call(
        respond,
        pltpu.VMEM((cols, height, 128), bf16),
        cols // step,
        [blocks((step * SHARE, n_out), 0), whole(given.shape)],
        blocks((step, height, 128), 0),
        (basis_out, given),
        6 * basis_out.size * train,
        16,
    )
    response = sum_of(exchange(message, COL), n)
    return [response[k] for k in range(n)]


def body(basis_out, basis_in, eig_damped, query_left, query_right, train_left, train_right):
    cols = lax.axis_size(COL)
    rank, train = query_right.shape[1], train_right.shape[1]
    n_out, _ = eig_damped.shape
    struct = jax.ShapeDtypeStruct

    step = 4
    n = (rank + train) // 128
    height = n * SHARE + tail_of(n)
    wide = step // 2 * 128
    given = jnp.concatenate([query_right, train_right], axis=1).T
    given = jnp.concatenate([given, given], axis=1)
    extra = rank // 128 * SHARE
    message = call(
        rotate_in,
        pltpu.VMEM((4, 2, 4, height + extra, 128), bf16),
        cols // step,
        [
            blocks((basis_in.shape[0], wide), 1),
            whole(given.shape),
            whole(query_left.shape),
        ],
        pl.BlockSpec((1, 2, 2, height + extra, 128), lambda i: (i // 2, 0, i % 2, 0, 0)),
        (pltpu.with_memory_space_constraint(basis_in, pltpu.HBM), given, query_left),
        4 * basis_in.size * (rank + train),
        16,
    ).reshape(cols, height + extra, 128)
    got = exchange(message, COL)

    message = message_of(sum_of(got, n))
    other = lax.ppermute(message, "col_1", ring("col_1", 1))
    is_first = lax.axis_index("col_1") == 0
    first = jnp.where(is_first, message, other)
    second = jnp.where(is_first, other, message)
    first, second, got = lax.optimization_barrier((first, second, got))
    firsts = jnp.stack(around(first, "col_0"))
    seconds = jnp.stack(around(second, "col_2"))
    firsts, seconds = lax.optimization_barrier((firsts, seconds))
    pieces = around(firsts, "col_2") + around(seconds, "col_0")

    high, low = split(basis_out)
    query = got[:, n * SHARE : n * SHARE + extra].reshape(cols, -1, SHARE, 128)
    query = query.transpose(0, 2, 1, 3).reshape(cols * SHARE, rank)
    rot_left = multiply(high, query, FIRST) + multiply(low, query, FIRST)
    rot_left = both_halves(summed_over_chips(my_half_summed(rot_left), (firsts, seconds)))
    high, low = split(rot_left)
    left = jnp.concatenate([high, low, high], axis=1)

    place = jnp.stack([lax.axis_index("col_0"), lax.axis_index("col_2")]).astype(jnp.int32)
    contrib = pl.pallas_call(
        apply_piece,
        out_shape=struct((n_out, train), f32),
        in_specs=[pl.BlockSpec(memory_space=pltpu.SMEM)]
        + [pl.BlockSpec(memory_space=k) for k in [pltpu.VMEM, pl.ANY] + [pltpu.VMEM] * 8],
        scratch_shapes=[
            pltpu.VMEM((2, 3 * rank, wide), bf16),
            pltpu.VMEM((2, train, 3 * wide), bf16),
            pltpu.VMEM((8, n_out, 256), f32),
            pltpu.SemaphoreType.DMA((16,)),
        ],
        cost_estimate=pl.CostEstimate(
            flops=6 * eig_damped.size * (rank + train),
            transcendentals=0,
            bytes_accessed=eig_damped.size * 4,
        ),
        compiler_params=pltpu.CompilerParams(vmem_limit_bytes=18 * 2**20),
        name="apply_piece",
    )(place, left, pltpu.with_memory_space_constraint(eig_damped, pltpu.HBM), *pieces)
    applied = both_halves(summed_in_turn(my_half_summed(contrib)))
    response = jnp.concatenate(respond_to(basis_out, applied), axis=1)
    scores = jnp.sum(train_left.astype(f32) * response, axis=0).reshape(-1, 128)
    scores = jnp.sum(to_everyone(scores, COL), axis=0)
    scores = jnp.sum(to_everyone(scores, ROW), axis=0)
    return response, scores.reshape(-1)


def solution(mesh):
    finer = Mesh(mesh.devices.reshape(4, 2, 4, 2, 4), ROW_COL)
    placed = (
        P(ROW, COL),
        P(COL, ROW),
        P(COL, ROW),
        P(ROW_COL, None),
        P(COL, None),
        P(ROW_COL, None),
        P(COL, None),
    )

    return jax.shard_map(
        body, mesh=finer, in_specs=placed, out_specs=(P(ROW_COL, None), P()), check_vma=False
    )
```

```python
import jax
import jax.numpy as jnp
from jax import lax
from jax.experimental import pallas as pl
from jax.experimental.pallas import tpu as pltpu
from jax.sharding import Mesh
from jax.sharding import PartitionSpec as P

COL = ("col_0", "col_1", "col_2")
ROW = ("row_0", "row_1")
ROW_COL = ROW + COL


SPAN = 250.0
HALF = 125.0
SHARE = 64
f32, bf16 = jnp.float32, jnp.bfloat16


def exchange(pieces, axis):
    return lax.all_to_all(pieces, axis, split_axis=0, concat_axis=0, tiled=True)


def to_everyone(array, axis):
    return exchange(jnp.broadcast_to(array, (lax.axis_size(axis), *array.shape)), axis)


def ring(axis, step):
    n = lax.axis_size(axis)
    return [(k, (k + step) % n) for k in range(n)]


def tail_of(n):
    return 8 if n <= 4 else 16


def levels_of(block, axis):
    most = jnp.max(jnp.abs(block), axis=axis, keepdims=True)
    level = jnp.ceil(jnp.log2(jnp.maximum(most, 1e-36)) * 8.0) * 0.125
    return level, jnp.floor(level)


def code_of(block, level):
    size = jnp.exp2(jnp.abs(block) * (jnp.exp2(-level) * SPAN) - HALF)
    return jnp.where(block < 0, -size, size).astype(bf16)


def value_of(code, scale):
    code = code.astype(f32)
    size = (jnp.log2(jnp.abs(code)) + HALF) * scale
    return jnp.where(code < 0, -size, size)


def put_blocks(out, lead, parts, plain=()):
    tail = tail_of(len(parts))
    out = out.at[lead]
    rows = jnp.zeros((tail, 128), f32)
    at = lax.broadcasted_iota(jnp.int32, (tail, 128), 0)
    for k, part in enumerate(parts):
        level, first = levels_of(part, 0)
        out[pl.ds(k * SHARE, SHARE), :] = code_of(part, level)
        rows = jnp.where(at == k, first, rows)
        rows = jnp.where(at == k + tail // 2, level - first, rows)
    for k, part in enumerate(plain):
        out[pl.ds((len(parts) + k) * SHARE, SHARE), :] = part
    out[pl.ds(out.shape[0] - tail, tail), :] = rows.astype(bf16)


def message_of(blocks):
    level, first = levels_of(blocks, 1)
    code = code_of(blocks, level).reshape(-1, 128)
    pad = ((0, tail_of(blocks.shape[0]) // 2 - blocks.shape[0]), (0, 0))
    rows = [jnp.pad(a[:, 0], pad).astype(bf16) for a in (first, level - first)]
    return jnp.concatenate([code, *rows], axis=0)


def sum_of(got, n):
    at = got.shape[1] - tail_of(n)
    half = at + tail_of(n) // 2
    level = got[:, at : at + n].astype(f32) + got[:, half : half + n].astype(f32)
    scale = jnp.exp2(level)[:, :, None] * (1.0 / SPAN)
    return jnp.sum(value_of(got[:, : n * SHARE].reshape(-1, n, SHARE, 128), scale), axis=0)


def halves(array):
    high = array.astype(bf16)
    return high, (array - high.astype(f32)).astype(bf16)


def split(array):
    high = lax.reduce_precision(array, 8, 7)
    return high.astype(bf16), (array - high).astype(bf16)


def multiply(left, right, dims):
    return lax.dot_general(left, right, (dims, ((), ())), preferred_element_type=f32)


FIRST, PLAIN, LAST = ((0,), (0,)), ((1,), (0,)), ((1,), (1,))


def call(kernel, out, grid, ins, outs, args, flops, vmem, scratch=()):
    size = sum(a.size * a.dtype.itemsize for a in args)
    return pl.pallas_call(
        kernel,
        out_shape=out,
        grid=(grid,),
        in_specs=ins,
        out_specs=outs,
        scratch_shapes=scratch,
        cost_estimate=pl.CostEstimate(flops=flops, transcendentals=0, bytes_accessed=size),
        compiler_params=pltpu.CompilerParams(vmem_limit_bytes=vmem * 2**20),
    )(*args)


def whole(shape):
    return pl.BlockSpec(shape, lambda i: (0,) * len(shape))


def blocks(shape, dim):
    return pl.BlockSpec(shape, lambda i: tuple(i if k == dim else 0 for k in range(len(shape))))


OFFSETS = (0, 3, 1, 2)


def around(array, axis):
    return [array] + [lax.ppermute(array, axis, ring(axis, 4 - k)) for k in OFFSETS[1:]]


def rotate_in(basis, query_right, train_right, query, out, given):
    @pl.when(pl.program_id(0) == 0)
    def _():
        k, rank = query_right.shape
        for at in (0, k):
            given[pl.ds(0, rank), pl.ds(at, k)] = query_right[...].T
            given[pl.ds(rank, train_right.shape[1]), pl.ds(at, k)] = train_right[...].T

    right = jnp.concatenate(halves(basis[...]), axis=0)
    n = given.shape[0] // (2 * SHARE)
    plain = [query[:, k * 128 : (k + 1) * 128] for k in range(query.shape[1] // 128)]
    for h in range(2):
        rows = slice(h * n * SHARE, (h + 1) * n * SHARE)
        turned = multiply(given[rows, :], right, PLAIN)
        for d in range(out.shape[2]):
            cut = slice(d * 128, (d + 1) * 128)
            parts = [turned[k * SHARE : (k + 1) * SHARE, cut] for k in range(n)]
            put_blocks(out, (0, h, d), parts, plain)


def apply_piece(place, left, eig, *refs):
    firsts, seconds, (out, right, other, shares, done) = refs[:4], refs[4:8], refs[8:]
    n = (firsts[0].shape[1] - 16) // SHARE
    tall = right.shape[1] // 3
    copies = []
    for s in range(8):
        for t in range(2):
            group = lax.rem(place[0] + OFFSETS[s // 2], 4) * 4
            group += lax.rem(place[1] + OFFSETS[s % 2 * 2 + t], 4)
            lanes = pl.ds(pl.multiple_of(group * 128, 128), 128)
            into = shares.at[s, :, pl.ds(t * 128, 128)]
            copies.append(pltpu.make_async_copy(eig.at[:, lanes], into, done.at[s * 2 + t]))
            copies[-1].start()
    out[...] = jnp.zeros_like(out)
    for s in range(8):
        a, slot = s // 2, s % 2
        for t in range(2):
            b = s % 2 * 2 + t
            lanes = pl.ds(t * 128, 128)
            for h, got in enumerate((firsts[b].at[a], seconds[a].at[b])):
                rows = got[pl.ds(n * SHARE, 16), :].astype(f32)
                for k in range(n):
                    scale = jnp.exp2(rows[k : k + 1] + rows[k + 8 : k + 9]) * (1.0 / SPAN)
                    high, low = halves(value_of(got[pl.ds(k * SHARE, SHARE), :], scale))
                    at = (h * n + k) * SHARE
                    if at < tall:
                        right[slot, pl.ds(at, SHARE), lanes] = high
                        right[slot, pl.ds(tall + at, SHARE), lanes] = high
                        right[slot, pl.ds(2 * tall + at, SHARE), lanes] = low
                    else:
                        at = pl.ds(at - tall, SHARE)
                        other[slot, at, lanes] = high
                        other[slot, at, pl.ds(256 + t * 128, 128)] = high
                        other[slot, at, pl.ds(512 + t * 128, 128)] = low
        copies[2 * s].wait()
        copies[2 * s + 1].wait()
        precond = multiply(left[...], right[slot], PLAIN) / shares[s]
        high, low = halves(precond)
        out[...] += multiply(jnp.concatenate([high, low, high], axis=1), other[slot], LAST)


def respond(basis, given, out):
    high, low = halves(basis[...])
    partial = multiply(jnp.concatenate([high, low, high], axis=1), given[...], PLAIN)
    n = partial.shape[1] // 128
    for d in range(out.shape[0]):
        rows = slice(d * SHARE, (d + 1) * SHARE)
        put_blocks(out, d, [partial[rows, k * 128 : (k + 1) * 128] for k in range(n)])


def my_half_summed(array):
    core = lax.axis_index("row_1")
    rows = array.shape[0] // 2
    mine = lax.dynamic_slice_in_dim(array, core * rows, rows, 0)
    other = lax.dynamic_slice_in_dim(array, (1 - core) * rows, rows, 0)
    return mine + lax.ppermute(other, "row_1", ring("row_1", 1))


def both_halves(half):
    core = lax.axis_index("row_1")
    other = lax.ppermute(half, "row_1", ring("row_1", 1))
    return jnp.where(
        core == 0, jnp.concatenate([half, other], 0), jnp.concatenate([other, half], 0)
    )


def coded_columns(array, tail):
    cols = array.shape[1]
    parts = array.reshape(-1, SHARE, cols)
    level, first = levels_of(parts, 1)
    rows = [code_of(parts, level), first.astype(bf16), (level - first).astype(bf16)]
    rows.append(jnp.zeros((parts.shape[0], tail - 2, cols), bf16))
    return jnp.concatenate(rows, axis=1)


def column_values(message):
    level = message[:, SHARE].astype(f32) + message[:, SHARE + 1].astype(f32)
    return value_of(message[:, :SHARE], jnp.exp2(level)[:, None] * (1.0 / SPAN))


def summed_over_chips(array):
    message = coded_columns(array, 8)
    arrived = []
    for step in (2, 3, 1):
        arrived.append(lax.ppermute(message, "row_0", ring("row_0", step)))
    total = array
    for got in arrived:
        total += column_values(got).reshape(array.shape)
    return total


def summed_in_turn(array):
    me = lax.axis_index("row_0")
    chips = lax.axis_size("row_0")
    message = coded_columns(array, 8)
    total = lax.dynamic_slice_in_dim(array, me * SHARE, SHARE, 0)
    arrived = []
    for step in (1, 3, 2):
        piece = lax.dynamic_index_in_dim(message, lax.rem(me + step, chips), 0)
        arrived.append(lax.ppermute(piece, "row_0", ring("row_0", step)))
    for got in arrived:
        total += column_values(got)[0]
    pieces = lax.all_gather(coded_columns(total, 8), "row_0", axis=0, tiled=True)
    return column_values(pieces).reshape(array.shape)


def respond_to(basis_out, applied):
    cols = lax.axis_size(COL)
    n_out, train = applied.shape
    high, low = split(applied)
    given = jnp.concatenate([high, high, low], axis=0)
    n = train // 128
    height = n * SHARE + tail_of(n)
    step = 4
    message = call(
        respond,
        pltpu.VMEM((cols, height, 128), bf16),
        cols // step,
        [blocks((step * SHARE, n_out), 0), whole(given.shape)],
        blocks((step, height, 128), 0),
        (basis_out, given),
        6 * basis_out.size * train,
        16,
    )
    response = sum_of(exchange(message, COL), n)
    return [response[k] for k in range(n)]


def body(basis_out, basis_in, eig_damped, query_left, query_right, train_left, train_right):
    cols = lax.axis_size(COL)
    rank, train = query_right.shape[1], train_right.shape[1]
    n_out, _ = eig_damped.shape
    struct = jax.ShapeDtypeStruct

    step = 4
    n = (rank + train) // 128
    height = n * SHARE + tail_of(n)
    wide = step // 2 * 128
    extra = rank // 128 * SHARE
    message = call(
        rotate_in,
        pltpu.VMEM((4, 2, 4, height + extra, 128), bf16),
        cols // step,
        [
            blocks((basis_in.shape[0], wide), 1),
            whole(query_right.shape),
            whole(train_right.shape),
            whole(query_left.shape),
        ],
        pl.BlockSpec((1, 2, 2, height + extra, 128), lambda i: (i // 2, 0, i % 2, 0, 0)),
        (
            pltpu.with_memory_space_constraint(basis_in, pltpu.HBM),
            query_right,
            train_right,
            query_left,
        ),
        4 * basis_in.size * (rank + train),
        16,
        [pltpu.VMEM((rank + train, 2 * basis_in.shape[0]), bf16)],
    ).reshape(cols, height + extra, 128)
    got = exchange(message, COL)

    message = message_of(sum_of(got, n))
    other = lax.ppermute(message, "col_1", ring("col_1", 1))
    is_first = lax.axis_index("col_1") == 0
    first = jnp.where(is_first, message, other)
    second = jnp.where(is_first, other, message)
    first, second, got = lax.optimization_barrier((first, second, got))
    firsts = jnp.stack(around(first, "col_0"))
    seconds = jnp.stack(around(second, "col_2"))
    firsts, seconds = lax.optimization_barrier((firsts, seconds))
    pieces = around(firsts, "col_2") + around(seconds, "col_0")

    high, low = split(basis_out)
    query = got[:, n * SHARE : n * SHARE + extra].reshape(cols, -1, SHARE, 128)
    query = query.transpose(0, 2, 1, 3).reshape(cols * SHARE, rank)
    rot_left = multiply(high, query, FIRST) + multiply(low, query, FIRST)
    rot_left = both_halves(summed_over_chips(my_half_summed(rot_left)))
    high, low = split(rot_left)
    left = jnp.concatenate([high, low, high], axis=1)

    place = jnp.stack([lax.axis_index("col_0"), lax.axis_index("col_2")]).astype(jnp.int32)
    contrib = pl.pallas_call(
        apply_piece,
        out_shape=struct((n_out, train), f32),
        in_specs=[pl.BlockSpec(memory_space=pltpu.SMEM)]
        + [pl.BlockSpec(memory_space=k) for k in [pltpu.VMEM, pl.ANY] + [pltpu.VMEM] * 8],
        scratch_shapes=[
            pltpu.VMEM((2, 3 * rank, wide), bf16),
            pltpu.VMEM((2, train, 3 * wide), bf16),
            pltpu.VMEM((8, n_out, 256), f32),
            pltpu.SemaphoreType.DMA((16,)),
        ],
        cost_estimate=pl.CostEstimate(
            flops=6 * eig_damped.size * (rank + train),
            transcendentals=0,
            bytes_accessed=eig_damped.size * 4,
        ),
        compiler_params=pltpu.CompilerParams(vmem_limit_bytes=12 * 2**20),
        name="apply_piece",
    )(place, left, pltpu.with_memory_space_constraint(eig_damped, pltpu.HBM), *pieces)
    applied = both_halves(summed_in_turn(my_half_summed(contrib)))
    response = jnp.concatenate(respond_to(basis_out, applied), axis=1)
    scores = jnp.sum(train_left.astype(f32) * response, axis=0).reshape(-1, 128)
    scores = jnp.sum(to_everyone(scores, COL), axis=0)
    scores = jnp.sum(to_everyone(scores, ROW), axis=0)
    return response, scores.reshape(-1)


def solution(mesh):
    finer = Mesh(mesh.devices.reshape(4, 2, 4, 2, 4), ROW_COL)
    placed = (
        P(ROW, COL),
        P(COL, ROW),
        P(COL, ROW),
        P(ROW_COL, None),
        P(COL, None),
        P(ROW_COL, None),
        P(COL, None),
    )

    return jax.shard_map(
        body, mesh=finer, in_specs=placed, out_specs=(P(ROW_COL, None), P()), check_vma=False
    )
```

```python
import jax
import jax.numpy as jnp
from jax import lax
from jax.experimental import pallas as pl
from jax.experimental.pallas import tpu as pltpu
from jax.sharding import Mesh
from jax.sharding import PartitionSpec as P

COL = ("col_0", "col_1", "col_2")
ROW = ("row_0", "row_1")
ROW_COL = ROW + COL


SPAN = 250.0
HALF = 125.0
SHARE = 64
f32, bf16 = jnp.float32, jnp.bfloat16


def exchange(pieces, axis):
    return lax.all_to_all(pieces, axis, split_axis=0, concat_axis=0, tiled=True)


def to_everyone(array, axis):
    return exchange(jnp.broadcast_to(array, (lax.axis_size(axis), *array.shape)), axis)


def ring(axis, step):
    n = lax.axis_size(axis)
    return [(k, (k + step) % n) for k in range(n)]


def tail_of(n):
    return 8 if n <= 4 else 16


def levels_of(block, axis):
    most = jnp.max(jnp.abs(block), axis=axis, keepdims=True)
    level = jnp.ceil(jnp.log2(jnp.maximum(most, 1e-36)) * 8.0) * 0.125
    return level, jnp.floor(level)


def code_of(block, level):
    size = jnp.exp2(jnp.abs(block) * (jnp.exp2(-level) * SPAN) - HALF)
    return jnp.where(block < 0, -size, size).astype(bf16)


def value_of(code, scale):
    code = code.astype(f32)
    size = (jnp.log2(jnp.abs(code)) + HALF) * scale
    return jnp.where(code < 0, -size, size)


def put_blocks(out, lead, parts, plain=()):
    tail = tail_of(len(parts))
    out = out.at[lead]
    rows = jnp.zeros((tail, 128), f32)
    at = lax.broadcasted_iota(jnp.int32, (tail, 128), 0)
    for k, part in enumerate(parts):
        level, first = levels_of(part, 0)
        out[pl.ds(k * SHARE, SHARE), :] = code_of(part, level)
        rows = jnp.where(at == k, first, rows)
        rows = jnp.where(at == k + tail // 2, level - first, rows)
    for k, part in enumerate(plain):
        out[pl.ds((len(parts) + k) * SHARE, SHARE), :] = part
    out[pl.ds(out.shape[0] - tail, tail), :] = rows.astype(bf16)


def message_of(blocks):
    level, first = levels_of(blocks, 1)
    code = code_of(blocks, level).reshape(-1, 128)
    pad = ((0, tail_of(blocks.shape[0]) // 2 - blocks.shape[0]), (0, 0))
    rows = [jnp.pad(a[:, 0], pad).astype(bf16) for a in (first, level - first)]
    return jnp.concatenate([code, *rows], axis=0)


def sum_of(got, n):
    at = got.shape[1] - tail_of(n)
    half = at + tail_of(n) // 2
    level = got[:, at : at + n].astype(f32) + got[:, half : half + n].astype(f32)
    scale = jnp.exp2(level)[:, :, None] * (1.0 / SPAN)
    return jnp.sum(value_of(got[:, : n * SHARE].reshape(-1, n, SHARE, 128), scale), axis=0)


def halves(array):
    high = array.astype(bf16)
    return high, (array - high.astype(f32)).astype(bf16)


def split(array):
    high = lax.reduce_precision(array, 8, 7)
    return high.astype(bf16), (array - high).astype(bf16)


def multiply(left, right, dims):
    return lax.dot_general(left, right, (dims, ((), ())), preferred_element_type=f32)


FIRST, PLAIN, LAST = ((0,), (0,)), ((1,), (0,)), ((1,), (1,))


def call(kernel, out, grid, ins, outs, args, flops, vmem, scratch=()):
    size = sum(a.size * a.dtype.itemsize for a in args)
    return pl.pallas_call(
        kernel,
        out_shape=out,
        grid=(grid,),
        in_specs=ins,
        out_specs=outs,
        scratch_shapes=scratch,
        cost_estimate=pl.CostEstimate(flops=flops, transcendentals=0, bytes_accessed=size),
        compiler_params=pltpu.CompilerParams(vmem_limit_bytes=vmem * 2**20),
    )(*args)


def whole(shape):
    return pl.BlockSpec(shape, lambda i: (0,) * len(shape))


def blocks(shape, dim):
    return pl.BlockSpec(shape, lambda i: tuple(i if k == dim else 0 for k in range(len(shape))))


OFFSETS = (0, 3, 1, 2)


def around(array, axis):
    return [array] + [lax.ppermute(array, axis, ring(axis, 4 - k)) for k in OFFSETS[1:]]


def rotate_in(basis, query_right, train_right, query, out, given):
    @pl.when(pl.program_id(0) == 0)
    def _():
        k, rank = query_right.shape
        for at in (0, k):
            given[pl.ds(0, rank), pl.ds(at, k)] = query_right[...].T
            given[pl.ds(rank, train_right.shape[1]), pl.ds(at, k)] = train_right[...].T

    right = jnp.concatenate(halves(basis[...]), axis=0)
    n = given.shape[0] // (2 * SHARE)
    plain = [query[:, k * 128 : (k + 1) * 128] for k in range(query.shape[1] // 128)]
    for h in range(2):
        rows = slice(h * n * SHARE, (h + 1) * n * SHARE)
        turned = multiply(given[rows, :], right, PLAIN)
        for d in range(out.shape[2]):
            cut = slice(d * 128, (d + 1) * 128)
            parts = [turned[k * SHARE : (k + 1) * SHARE, cut] for k in range(n)]
            put_blocks(out, (0, h, d), parts, plain)


def apply_piece(place, left, eig, *refs):
    firsts, seconds, (out, right, other, shares, done) = refs[:4], refs[4:8], refs[8:]
    n = (firsts[0].shape[1] - 16) // SHARE
    tall = right.shape[1] // 3
    copies = []
    for s in range(8):
        for t in range(2):
            group = lax.rem(place[0] + OFFSETS[s // 2], 4) * 4
            group += lax.rem(place[1] + OFFSETS[s % 2 * 2 + t], 4)
            lanes = pl.ds(pl.multiple_of(group * 128, 128), 128)
            into = shares.at[s, :, pl.ds(t * 128, 128)]
            copies.append(pltpu.make_async_copy(eig.at[:, lanes], into, done.at[s * 2 + t]))
            copies[-1].start()
    out[...] = jnp.zeros_like(out)
    for s in range(8):
        a, slot = s // 2, s % 2
        for t in range(2):
            b = s % 2 * 2 + t
            lanes = pl.ds(t * 128, 128)
            for h, got in enumerate((firsts[b].at[a], seconds[a].at[b])):
                rows = got[pl.ds(n * SHARE, 16), :].astype(f32)
                for k in range(n):
                    scale = jnp.exp2(rows[k : k + 1] + rows[k + 8 : k + 9]) * (1.0 / SPAN)
                    high, low = halves(value_of(got[pl.ds(k * SHARE, SHARE), :], scale))
                    at = (h * n + k) * SHARE
                    if at < tall:
                        right[slot, pl.ds(at, SHARE), lanes] = high
                        right[slot, pl.ds(tall + at, SHARE), lanes] = high
                        right[slot, pl.ds(2 * tall + at, SHARE), lanes] = low
                    else:
                        at = pl.ds(at - tall, SHARE)
                        other[slot, at, lanes] = high
                        other[slot, at, pl.ds(256 + t * 128, 128)] = high
                        other[slot, at, pl.ds(512 + t * 128, 128)] = low
        copies[2 * s].wait()
        copies[2 * s + 1].wait()
        precond = multiply(left[...], right[slot], PLAIN) / shares[s]
        high, low = halves(precond)
        out[...] += multiply(jnp.concatenate([high, low, high], axis=1), other[slot], LAST)


def respond(basis, given, out):
    high, low = halves(basis[...])
    partial = multiply(jnp.concatenate([high, low, high], axis=1), given[...], PLAIN)
    n = partial.shape[1] // 128
    for d in range(out.shape[0]):
        rows = slice(d * SHARE, (d + 1) * SHARE)
        put_blocks(out, d, [partial[rows, k * 128 : (k + 1) * 128] for k in range(n)])


def my_half_summed(array, core):
    rows = array.shape[0] // 2
    mine = lax.dynamic_slice_in_dim(array, core * rows, rows, 0)
    other = lax.dynamic_slice_in_dim(array, (1 - core) * rows, rows, 0)
    return mine + lax.ppermute(other, "row_1", ring("row_1", 1))


def both_halves(half, core):
    other = lax.ppermute(half, "row_1", ring("row_1", 1))
    return jnp.where(
        core == 0, jnp.concatenate([half, other], 0), jnp.concatenate([other, half], 0)
    )


def coded_columns(array, tail):
    cols = array.shape[1]
    parts = array.reshape(-1, SHARE, cols)
    level, first = levels_of(parts, 1)
    rows = [code_of(parts, level), first.astype(bf16), (level - first).astype(bf16)]
    rows.append(jnp.zeros((parts.shape[0], tail - 2, cols), bf16))
    return jnp.concatenate(rows, axis=1)


def column_values(message):
    level = message[:, SHARE].astype(f32) + message[:, SHARE + 1].astype(f32)
    return value_of(message[:, :SHARE], jnp.exp2(level)[:, None] * (1.0 / SPAN))


def summed_over_chips(array):
    message = coded_columns(array, 8)
    arrived = []
    for step in (2, 3, 1):
        arrived.append(lax.ppermute(message, "row_0", ring("row_0", step)))
    total = array
    for got in arrived:
        total += column_values(got).reshape(array.shape)
    return total


def summed_in_turn(array):
    me = lax.axis_index("row_0")
    chips = lax.axis_size("row_0")
    message = coded_columns(array, 8)
    total = lax.dynamic_slice_in_dim(array, me * SHARE, SHARE, 0)
    arrived = []
    for step in (2, 3, 1):
        piece = lax.dynamic_index_in_dim(message, lax.rem(me + step, chips), 0)
        arrived.append(lax.ppermute(piece, "row_0", ring("row_0", step)))
    for got in arrived:
        total += column_values(got)[0]
    pieces = lax.all_gather(coded_columns(total, 8), "row_0", axis=0, tiled=True)
    return column_values(pieces).reshape(array.shape)


def respond_to(basis_out, applied):
    cols = lax.axis_size(COL)
    n_out, train = applied.shape
    high, low = split(applied)
    given = jnp.concatenate([high, high, low], axis=0)
    n = train // 128
    height = n * SHARE + tail_of(n)
    step = 4
    message = call(
        respond,
        pltpu.VMEM((cols, height, 128), bf16),
        cols // step,
        [blocks((step * SHARE, n_out), 0), whole(given.shape)],
        blocks((step, height, 128), 0),
        (basis_out, given),
        6 * basis_out.size * train,
        16,
    )
    response = sum_of(exchange(message, COL), n)
    return [response[k] for k in range(n)]


def body(basis_out, basis_in, eig_damped, query_left, query_right, train_left, train_right):
    cols = lax.axis_size(COL)
    rank, train = query_right.shape[1], train_right.shape[1]
    n_out, _ = eig_damped.shape
    struct = jax.ShapeDtypeStruct
    core, query_left = lax.optimization_barrier((lax.axis_index("row_1"), query_left))

    step = 4
    n = (rank + train) // 128
    height = n * SHARE + tail_of(n)
    wide = step // 2 * 128
    extra = rank // 128 * SHARE
    message = call(
        rotate_in,
        pltpu.VMEM((4, 2, 4, height + extra, 128), bf16),
        cols // step,
        [
            blocks((basis_in.shape[0], wide), 1),
            whole(query_right.shape),
            whole(train_right.shape),
            whole(query_left.shape),
        ],
        pl.BlockSpec((1, 2, 2, height + extra, 128), lambda i: (i // 2, 0, i % 2, 0, 0)),
        (
            pltpu.with_memory_space_constraint(basis_in, pltpu.HBM),
            query_right,
            train_right,
            query_left,
        ),
        4 * basis_in.size * (rank + train),
        16,
        [pltpu.VMEM((rank + train, 2 * basis_in.shape[0]), bf16)],
    ).reshape(cols, height + extra, 128)
    core, got = lax.optimization_barrier((core, exchange(message, COL)))

    message, got = lax.optimization_barrier((message_of(sum_of(got, n)), got))
    other = lax.ppermute(message, "col_1", ring("col_1", 1))
    is_first = lax.axis_index("col_1") == 0
    first = jnp.where(is_first, message, other)
    second = jnp.where(is_first, other, message)
    firsts = jnp.stack(around(first, "col_0"))
    seconds = jnp.stack(around(second, "col_2"))
    firsts, seconds = lax.optimization_barrier((firsts, seconds))
    pieces = around(firsts, "col_2") + around(seconds, "col_0")

    high, low = split(basis_out)
    query = got[:, n * SHARE : n * SHARE + extra].reshape(cols, -1, SHARE, 128)
    query = query.transpose(0, 2, 1, 3).reshape(cols * SHARE, rank)
    rot_left = multiply(high, query, FIRST) + multiply(low, query, FIRST)
    rot_left = both_halves(summed_over_chips(my_half_summed(rot_left, core)), core)
    high, low = split(rot_left)
    left = jnp.concatenate([high, low, high], axis=1)

    place = jnp.stack([lax.axis_index("col_0"), lax.axis_index("col_2")]).astype(jnp.int32)
    contrib = pl.pallas_call(
        apply_piece,
        out_shape=struct((n_out, train), f32),
        in_specs=[pl.BlockSpec(memory_space=pltpu.SMEM)]
        + [pl.BlockSpec(memory_space=k) for k in [pltpu.VMEM, pl.ANY] + [pltpu.VMEM] * 8],
        scratch_shapes=[
            pltpu.VMEM((2, 3 * rank, wide), bf16),
            pltpu.VMEM((2, train, 3 * wide), bf16),
            pltpu.VMEM((8, n_out, 256), f32),
            pltpu.SemaphoreType.DMA((16,)),
        ],
        cost_estimate=pl.CostEstimate(
            flops=6 * eig_damped.size * (rank + train),
            transcendentals=0,
            bytes_accessed=eig_damped.size * 4,
        ),
        compiler_params=pltpu.CompilerParams(vmem_limit_bytes=12 * 2**20),
        name="apply_piece",
    )(place, left, pltpu.with_memory_space_constraint(eig_damped, pltpu.HBM), *pieces)
    applied = both_halves(summed_in_turn(my_half_summed(contrib, core)), core)
    response = jnp.concatenate(respond_to(basis_out, applied), axis=1)
    scores = jnp.sum(train_left.astype(f32) * response, axis=0).reshape(-1, 128)
    scores = jnp.sum(to_everyone(scores, COL), axis=0)
    scores = jnp.sum(to_everyone(scores, ROW), axis=0)
    return response, scores.reshape(-1)


def solution(mesh):
    finer = Mesh(mesh.devices.reshape(4, 2, 4, 2, 4), ROW_COL)
    placed = (
        P(ROW, COL),
        P(COL, ROW),
        P(COL, ROW),
        P(ROW_COL, None),
        P(COL, None),
        P(ROW_COL, None),
        P(COL, None),
    )

    return jax.shard_map(
        body, mesh=finer, in_specs=placed, out_specs=(P(ROW_COL, None), P()), check_vma=False
    )
```

```python
import jax
import jax.numpy as jnp
from jax import lax
from jax.experimental import pallas as pl
from jax.experimental.pallas import tpu as pltpu
from jax.sharding import Mesh
from jax.sharding import PartitionSpec as P

COL = ("col_0", "col_1", "col_2")
ROW = ("row_0", "row_1")
ROW_COL = ROW + COL


SPAN = 250.0
HALF = 125.0
SHARE = 64
f32, bf16 = jnp.float32, jnp.bfloat16


def exchange(pieces, axis):
    return lax.all_to_all(pieces, axis, split_axis=0, concat_axis=0, tiled=True)


def to_everyone(array, axis):
    return exchange(jnp.broadcast_to(array, (lax.axis_size(axis), *array.shape)), axis)


def ring(axis, step):
    n = lax.axis_size(axis)
    return [(k, (k + step) % n) for k in range(n)]


def tail_of(n):
    return 8 if n <= 4 else 16


def levels_of(block, axis):
    most = jnp.max(jnp.abs(block), axis=axis, keepdims=True)
    level = jnp.ceil(jnp.log2(jnp.maximum(most, 1e-36)) * 8.0) * 0.125
    return level, jnp.floor(level)


def code_of(block, level):
    size = jnp.exp2(jnp.abs(block) * (jnp.exp2(-level) * SPAN) - HALF)
    return jnp.where(block < 0, -size, size).astype(bf16)


def value_of(code, scale):
    code = code.astype(f32)
    size = (jnp.log2(jnp.abs(code)) + HALF) * scale
    return jnp.where(code < 0, -size, size)


def put_blocks(out, lead, parts, plain=()):
    tail = tail_of(len(parts))
    out = out.at[lead]
    rows = jnp.zeros((tail, 128), f32)
    at = lax.broadcasted_iota(jnp.int32, (tail, 128), 0)
    for k, part in enumerate(parts):
        level, first = levels_of(part, 0)
        out[pl.ds(k * SHARE, SHARE), :] = code_of(part, level)
        rows = jnp.where(at == k, first, rows)
        rows = jnp.where(at == k + tail // 2, level - first, rows)
    for k, part in enumerate(plain):
        out[pl.ds((len(parts) + k) * SHARE, SHARE), :] = part
    out[pl.ds(out.shape[0] - tail, tail), :] = rows.astype(bf16)


def message_of(blocks):
    level, first = levels_of(blocks, 1)
    code = code_of(blocks, level).reshape(-1, 128)
    pad = ((0, tail_of(blocks.shape[0]) // 2 - blocks.shape[0]), (0, 0))
    rows = [jnp.pad(a[:, 0], pad).astype(bf16) for a in (first, level - first)]
    return jnp.concatenate([code, *rows], axis=0)


def sum_of(got, n):
    at = got.shape[1] - tail_of(n)
    half = at + tail_of(n) // 2
    level = got[:, at : at + n].astype(f32) + got[:, half : half + n].astype(f32)
    scale = jnp.exp2(level)[:, :, None] * (1.0 / SPAN)
    return jnp.sum(value_of(got[:, : n * SHARE].reshape(-1, n, SHARE, 128), scale), axis=0)


def halves(array):
    high = array.astype(bf16)
    return high, (array - high.astype(f32)).astype(bf16)


def split(array):
    high = lax.reduce_precision(array, 8, 7)
    return high.astype(bf16), (array - high).astype(bf16)


def multiply(left, right, dims):
    return lax.dot_general(left, right, (dims, ((), ())), preferred_element_type=f32)


FIRST, PLAIN, LAST = ((0,), (0,)), ((1,), (0,)), ((1,), (1,))


def call(kernel, out, grid, ins, outs, args, flops, vmem, scratch=()):
    size = sum(a.size * a.dtype.itemsize for a in args)
    return pl.pallas_call(
        kernel,
        out_shape=out,
        grid=(grid,),
        in_specs=ins,
        out_specs=outs,
        scratch_shapes=scratch,
        cost_estimate=pl.CostEstimate(flops=flops, transcendentals=0, bytes_accessed=size),
        compiler_params=pltpu.CompilerParams(vmem_limit_bytes=vmem * 2**20),
    )(*args)


def whole(shape):
    return pl.BlockSpec(shape, lambda i: (0,) * len(shape))


def blocks(shape, dim):
    return pl.BlockSpec(shape, lambda i: tuple(i if k == dim else 0 for k in range(len(shape))))


OFFSETS = (0, 3, 1, 2)


def around(array, axis):
    return [array] + [lax.ppermute(array, axis, ring(axis, 4 - k)) for k in OFFSETS[1:]]


def rotate_in(basis, query_right, train_right, query, out, given):
    @pl.when(pl.program_id(0) == 0)
    def _():
        k, rank = query_right.shape
        for at in (0, k):
            given[pl.ds(0, rank), pl.ds(at, k)] = query_right[...].T
            given[pl.ds(rank, train_right.shape[1]), pl.ds(at, k)] = train_right[...].T

    right = jnp.concatenate(halves(basis[...]), axis=0)
    n = given.shape[0] // (2 * SHARE)
    plain = [query[:, k * 128 : (k + 1) * 128] for k in range(query.shape[1] // 128)]
    for h in range(2):
        rows = slice(h * n * SHARE, (h + 1) * n * SHARE)
        turned = multiply(given[rows, :], right, PLAIN)
        for d in range(out.shape[2]):
            cut = slice(d * 128, (d + 1) * 128)
            parts = [turned[k * SHARE : (k + 1) * SHARE, cut] for k in range(n)]
            put_blocks(out, (0, h, d), parts, plain)


def apply_piece(place, left, eig, *refs):
    firsts, seconds, (out, right, other, shares, done) = refs[:4], refs[4:8], refs[8:]
    n = (firsts[0].shape[1] - 16) // SHARE
    tall = right.shape[1] // 3
    copies = []
    for s in range(8):
        for t in range(2):
            group = lax.rem(place[0] + OFFSETS[s // 2], 4) * 4
            group += lax.rem(place[1] + OFFSETS[s % 2 * 2 + t], 4)
            lanes = pl.ds(pl.multiple_of(group * 128, 128), 128)
            into = shares.at[s, :, pl.ds(t * 128, 128)]
            copies.append(pltpu.make_async_copy(eig.at[:, lanes], into, done.at[s * 2 + t]))
            copies[-1].start()
    out[...] = jnp.zeros_like(out)
    for s in range(8):
        a, slot = s // 2, s % 2
        for t in range(2):
            b = s % 2 * 2 + t
            lanes = pl.ds(t * 128, 128)
            for h, got in enumerate((firsts[b].at[a], seconds[a].at[b])):
                rows = got[pl.ds(n * SHARE, 16), :].astype(f32)
                for k in range(n):
                    scale = jnp.exp2(rows[k : k + 1] + rows[k + 8 : k + 9]) * (1.0 / SPAN)
                    high, low = halves(value_of(got[pl.ds(k * SHARE, SHARE), :], scale))
                    at = (h * n + k) * SHARE
                    if at < tall:
                        right[slot, pl.ds(at, SHARE), lanes] = high
                        right[slot, pl.ds(tall + at, SHARE), lanes] = high
                        right[slot, pl.ds(2 * tall + at, SHARE), lanes] = low
                    else:
                        at = pl.ds(at - tall, SHARE)
                        other[slot, at, lanes] = high
                        other[slot, at, pl.ds(256 + t * 128, 128)] = high
                        other[slot, at, pl.ds(512 + t * 128, 128)] = low
        copies[2 * s].wait()
        copies[2 * s + 1].wait()
        precond = multiply(left[...], right[slot], PLAIN) / shares[s]
        high, low = halves(precond)
        out[...] += multiply(jnp.concatenate([high, low, high], axis=1), other[slot], LAST)


def respond(basis, given, out):
    high, low = halves(basis[...])
    partial = multiply(jnp.concatenate([high, low, high], axis=1), given[...], PLAIN)
    n = partial.shape[1] // 128
    for d in range(out.shape[0]):
        rows = slice(d * SHARE, (d + 1) * SHARE)
        put_blocks(out, d, [partial[rows, k * 128 : (k + 1) * 128] for k in range(n)])


def my_half_summed(array, core):
    rows = array.shape[0] // 2
    mine = lax.dynamic_slice_in_dim(array, core * rows, rows, 0)
    other = lax.dynamic_slice_in_dim(array, (1 - core) * rows, rows, 0)
    return mine + lax.ppermute(other, "row_1", ring("row_1", 1))


def both_halves(half, core):
    other = lax.ppermute(half, "row_1", ring("row_1", 1))
    return jnp.where(
        core == 0, jnp.concatenate([half, other], 0), jnp.concatenate([other, half], 0)
    )


def coded_columns(array, tail):
    cols = array.shape[1]
    parts = array.reshape(-1, SHARE, cols)
    level, first = levels_of(parts, 1)
    rows = [code_of(parts, level), first.astype(bf16), (level - first).astype(bf16)]
    rows.append(jnp.zeros((parts.shape[0], tail - 2, cols), bf16))
    return jnp.concatenate(rows, axis=1)


def column_values(message):
    level = message[:, SHARE].astype(f32) + message[:, SHARE + 1].astype(f32)
    return value_of(message[:, :SHARE], jnp.exp2(level)[:, None] * (1.0 / SPAN))


def summed_over_chips(array):
    message = coded_columns(array, 8)
    arrived = []
    for step in (2, 3, 1):
        arrived.append(lax.ppermute(message, "row_0", ring("row_0", step)))
    total = array
    for got in arrived:
        total += column_values(got).reshape(array.shape)
    return total


def summed_in_turn(array):
    me = lax.axis_index("row_0")
    chips = lax.axis_size("row_0")
    message = coded_columns(array, 8)
    total = lax.dynamic_slice_in_dim(array, me * SHARE, SHARE, 0)
    arrived = []
    for step in (2, 3, 1):
        piece = lax.dynamic_index_in_dim(message, lax.rem(me + step, chips), 0)
        arrived.append(lax.ppermute(piece, "row_0", ring("row_0", step)))
    for got in arrived:
        total += column_values(got)[0]
    pieces = lax.all_gather(coded_columns(total, 8), "row_0", axis=0, tiled=True)
    return column_values(pieces).reshape(array.shape)


def respond_to(basis_out, applied):
    cols = lax.axis_size(COL)
    n_out, train = applied.shape
    high, low = split(applied)
    given = jnp.concatenate([high, high, low], axis=0)
    n = train // 128
    height = n * SHARE + tail_of(n)
    step = 4
    message = call(
        respond,
        pltpu.VMEM((cols, height, 128), bf16),
        cols // step,
        [blocks((step * SHARE, n_out), 0), whole(given.shape)],
        blocks((step, height, 128), 0),
        (basis_out, given),
        6 * basis_out.size * train,
        16,
    )
    response = sum_of(exchange(message, COL), n)
    return [response[k] for k in range(n)]


def body(basis_out, basis_in, eig_damped, query_left, query_right, train_left, train_right):
    cols = lax.axis_size(COL)
    rank, train = query_right.shape[1], train_right.shape[1]
    n_out, _ = eig_damped.shape
    struct = jax.ShapeDtypeStruct
    core, query_left = lax.optimization_barrier((lax.axis_index("row_1"), query_left))

    step = 4
    n = (rank + train) // 128
    height = n * SHARE + tail_of(n)
    wide = step // 2 * 128
    extra = rank // 128 * SHARE
    message = call(
        rotate_in,
        pltpu.VMEM((4, 2, 4, height + extra, 128), bf16),
        cols // step,
        [
            blocks((basis_in.shape[0], wide), 1),
            whole(query_right.shape),
            whole(train_right.shape),
            whole(query_left.shape),
        ],
        pl.BlockSpec((1, 2, 2, height + extra, 128), lambda i: (i // 2, 0, i % 2, 0, 0)),
        (
            pltpu.with_memory_space_constraint(basis_in, pltpu.HBM),
            query_right,
            train_right,
            query_left,
        ),
        4 * basis_in.size * (rank + train),
        16,
        [pltpu.VMEM((rank + train, 2 * basis_in.shape[0]), bf16)],
    ).reshape(cols, height + extra, 128)
    core, got = lax.optimization_barrier((core, exchange(message, COL)))

    message, got = lax.optimization_barrier((message_of(sum_of(got, n)), got))
    other = lax.ppermute(message, "col_1", ring("col_1", 1))
    is_first = lax.axis_index("col_1") == 0
    first = jnp.where(is_first, message, other)
    second = jnp.where(is_first, other, message)
    firsts = jnp.stack(around(first, "col_0"))
    seconds = jnp.stack(around(second, "col_2"))
    firsts, seconds = lax.optimization_barrier((firsts, seconds))
    pieces = around(firsts, "col_2") + around(seconds, "col_0")

    high, low = split(basis_out)
    query = got[:, n * SHARE : n * SHARE + extra].reshape(cols, -1, SHARE, 128)
    query = query.transpose(0, 2, 1, 3).reshape(cols * SHARE, rank)
    rot_left = multiply(high, query, FIRST) + multiply(low, query, FIRST)
    rot_left = both_halves(summed_over_chips(my_half_summed(rot_left, core)), core)
    high, low = split(rot_left)
    left = jnp.concatenate([high, low, high], axis=1)

    place = jnp.stack([lax.axis_index("col_0"), lax.axis_index("col_2")]).astype(jnp.int32)
    contrib = pl.pallas_call(
        apply_piece,
        out_shape=struct((n_out, train), f32),
        in_specs=[pl.BlockSpec(memory_space=pltpu.SMEM)]
        + [pl.BlockSpec(memory_space=k) for k in [pltpu.VMEM, pl.ANY] + [pltpu.VMEM] * 8],
        scratch_shapes=[
            pltpu.VMEM((2, 3 * rank, wide), bf16),
            pltpu.VMEM((2, train, 3 * wide), bf16),
            pltpu.VMEM((8, n_out, 256), f32),
            pltpu.SemaphoreType.DMA((16,)),
        ],
        cost_estimate=pl.CostEstimate(
            flops=6 * eig_damped.size * (rank + train),
            transcendentals=0,
            bytes_accessed=eig_damped.size * 4,
        ),
        compiler_params=pltpu.CompilerParams(vmem_limit_bytes=12 * 2**20),
        name="apply_piece",
    )(
        place,
        left,
        pltpu.with_memory_space_constraint(eig_damped, pltpu.HBM),
        *(
            pltpu.with_memory_space_constraint(piece, pltpu.HBM) if k % 4 == 0 else piece
            for k, piece in enumerate(pieces)
        ),
    )
    applied = both_halves(summed_in_turn(my_half_summed(contrib, core)), core)
    response = jnp.concatenate(respond_to(basis_out, applied), axis=1)
    scores = jnp.sum(train_left.astype(f32) * response, axis=0).reshape(-1, 128)
    scores = jnp.sum(to_everyone(scores, COL), axis=0)
    scores = jnp.sum(to_everyone(scores, ROW), axis=0)
    return response, scores.reshape(-1)


def solution(mesh):
    finer = Mesh(mesh.devices.reshape(4, 2, 4, 2, 4), ROW_COL)
    placed = (
        P(ROW, COL),
        P(COL, ROW),
        P(COL, ROW),
        P(ROW_COL, None),
        P(COL, None),
        P(ROW_COL, None),
        P(COL, None),
    )

    return jax.shard_map(
        body, mesh=finer, in_specs=placed, out_specs=(P(ROW_COL, None), P()), check_vma=False
    )
```
